32 devices in a mesh: grp: 2 (over y), ek: 8 (over z, x), per: 2 (over core).
Axes of the slice: x: 2, y: 2, z: 4, core: 2. Of those that a mesh axis runs over, the one named last changes fastest.
Arguments:
- retarded: bfloat16 [2, 32, 2, 640, 640], P('per', ('grp', 'ek')), parts along dimension 1, may hold values from -0.25 to 0.25
- scatter_root: float32 [2, 32, 640], P('per', ('grp', 'ek')), parts along dimension 1, may hold values from 0.2 to 1
- coupling: bfloat16 [640, 640], replicated, may hold values from -0.15625 to 0.15625
- source_index: int32 [16, 16], replicated, may hold values from 0 to 15
- kernel_weight: float32 [16, 16], replicated, may hold values from 0.02 to 0.5
Outputs:
- sigma_less: bfloat16 [2, 32, 2, 640, 640], P('per', 'grp', None, 'ek'), parts along dimension 1
The draws below stay inside these ranges and needn't reach their ends.
There are 2 independent parts, one for each index of `grp`. The reference program is written for one: setup_inputs(seed, part) draws one part's arguments, and reference() takes and returns one part's arrays. A program takes and returns all parts, laid end to end along the dimension named above; an argument that names none is the same for every part. Nothing has to cross between parts.
Inputs may be any that keep to these rules, and one draw needn't show every extreme that they name: `source_index`: source energy-k points of the phonon and roughness kernel.
All inputs are finite; a program needn't handle non-finite values.
Results may differ from the reference program's by a relative error of at most 0.0055.
Values may be sent and summed in bfloat16 or wider, within the bound.
A program may use at most 64 MiB of HBM per device.

```python
import math
import jax
import jax.numpy as jnp
from jax import lax

NS = 640
TAPS = 16
POINTS = 16
PERIODS = 2


def touch_ends(entries, rng, low, largest):
    index_at = [jax.random.randint(jax.random.fold_in(rng, axis), (), 0, length) for axis, length in enumerate(entries.shape)]
    longest = entries.shape.index(max(entries.shape))
    beside = index_at[:longest] + [(index_at[longest] + 1) % entries.shape[longest]] + index_at[longest + 1:]
    return entries.at[tuple(index_at)].set(low).at[tuple(beside)].set(largest)


def steps_of(stream_key, shape, shards, least, high):
    def one(axis_at, blocks):
        draws = jax.random.uniform(jax.random.fold_in(jax.random.fold_in(stream_key, 6), axis_at), (blocks,), jnp.float32, least / len(shards), high / len(shards))
        return jnp.repeat(jnp.exp(draws), shape[axis_at] // blocks).reshape((-1,) + (1,) * (len(shape) - axis_at - 1))

    loudness = one(*shards[0])
    for cut in shards[1:]:
        loudness = loudness * one(*cut)
    return loudness


def centred(rng, dims, deviation, limit, cuts=(), held_as=jnp.bfloat16):
    result = jax.random.normal(rng, dims, jnp.float32) * deviation
    if len(cuts) > 0:
        result = steps_of(rng, dims, cuts, -0.22, 0.18) * result
    return jnp.clip(result, min=-limit, max=limit).astype(held_as)


def setup_inputs(seed: int = 0, part: int = 0) -> dict:
    keys = jax.random.split(jax.random.key(seed), 6)
    part_keys = jax.random.split(jax.random.fold_in(keys[5], part), 6)
    retarded = centred(part_keys[0], (PERIODS, POINTS, 2, NS, NS), NS ** -0.5, 0.25, ((0, 2), (1, 8)))
    scatter_root = jnp.clip(jnp.exp(math.log(1.0) - 1.609438 * jax.random.uniform(part_keys[1], (PERIODS, POINTS, NS), jnp.float32) ** steps_of(part_keys[1], (PERIODS, POINTS, NS), ((0, 2), (1, 8)), -0.2, 0.2)), 0.2, 1.0)
    coupling = centred(keys[2], (NS, NS), (2 * NS) ** -0.5, 0.15625)
    source_index = touch_ends(jax.random.randint(keys[3], (POINTS, TAPS), 0, POINTS), jax.random.fold_in(keys[3], 1), 0, POINTS - 1).astype(jnp.int32)
    kernel_weight = jnp.clip(jnp.exp(jax.random.uniform(keys[4], (POINTS, TAPS), jnp.float32, math.log(0.02), math.log(0.5))), 0.02, 0.5)
    return {"retarded": retarded, "scatter_root": scatter_root, "coupling": coupling, "source_index": source_index, "kernel_weight": kernel_weight}


def product(former, latter):
    return jnp.dot(former, latter, preferred_element_type=jnp.float32)


def transposed_product(former, latter):
    return lax.dot_general(former, latter, (((1,), (1,)), ((), ())), preferred_element_type=jnp.float32)


def build_kernel(source_index, kernel_weight, total_points):
    targets = jnp.arange(total_points, dtype=jnp.int32)
    matches = (source_index[:, :, None] == targets[None, None, :]).astype(jnp.float32)
    return jnp.sum(kernel_weight[:, :, None] * matches, axis=1).astype(jnp.bfloat16)


def local_parts(real_g, imag_g, amplitude):
    root_real = (real_g * amplitude[None, :]).astype(jnp.bfloat16)
    root_imag = (imag_g * amplitude[None, :]).astype(jnp.bfloat16)
    local_real = transposed_product(root_real, root_real) + transposed_product(root_imag, root_imag)
    skewed = transposed_product(root_imag, root_real)
    return local_real, skewed - skewed.T


def coupled_parts(real_g, imag_g, coupling):
    return product(real_g, coupling).astype(jnp.bfloat16), product(imag_g, coupling).astype(jnp.bfloat16)


def advance(local_real, local_imag, coupled_real, coupled_imag, prev_real, prev_imag):
    carried_real = (product(coupled_real, prev_real) - product(coupled_imag, prev_imag)).astype(jnp.bfloat16)
    carried_imag = (product(coupled_real, prev_imag) + product(coupled_imag, prev_real)).astype(jnp.bfloat16)
    new_real = local_real + transposed_product(carried_real, coupled_real) + transposed_product(carried_imag, coupled_imag)
    new_imag = local_imag + transposed_product(carried_imag, coupled_real) - transposed_product(carried_real, coupled_imag)
    return jnp.stack([new_real.astype(jnp.bfloat16), new_imag.astype(jnp.bfloat16)])


def reference(retarded, scatter_root, coupling, source_index, kernel_weight):
    kernel = build_kernel(source_index, kernel_weight, POINTS)
    previous = jnp.zeros((POINTS, 2, NS, NS), jnp.bfloat16)
    outputs = []
    for period in range(PERIODS):
        def one_point(operands):
            green_pair, amplitude, before = operands
            local_real, local_imag = local_parts(green_pair[0], green_pair[1], amplitude)
            coupled_real, coupled_imag = coupled_parts(green_pair[0], green_pair[1], coupling)
            return advance(local_real, local_imag, coupled_real, coupled_imag, before[0], before[1])

        previous = lax.map(one_point, (retarded[period], scatter_root[period], previous))
        convolved = product(kernel, previous.reshape(POINTS, -1)).astype(jnp.bfloat16)
        outputs.append(convolved.reshape(POINTS, 2, NS, NS))
    return jnp.stack(outputs)
```

```python
import functools
import jax
import jax.numpy as jnp
from jax import lax
from jax.experimental import pallas as pl
from jax.experimental.pallas import tpu as pltpu
from jax.sharding import PartitionSpec as P


def shifted(array, axis, by):
    size = lax.axis_size(axis)
    pairs = [(i, i + by) for i in range(size) if 0 <= i + by < size]
    return lax.ppermute(array, axis, pairs)


def product(former, latter):
    return jnp.dot(former, latter, preferred_element_type=jnp.float32)


def transposed_product(former, latter):
    return lax.dot_general(
        former, latter, (((1,), (1,)), ((), ())), preferred_element_type=jnp.float32
    )


def build_kernel(source_index, kernel_weight, total_points):
    targets = jnp.arange(total_points, dtype=jnp.int32)
    matches = (source_index[:, :, None] == targets[None, None, :]).astype(jnp.float32)
    return jnp.sum(kernel_weight[:, :, None] * matches, axis=1).astype(jnp.bfloat16)


def local_parts(real_g, imag_g, amplitude):
    root_real = (real_g * amplitude[None, :]).astype(jnp.bfloat16)
    root_imag = (imag_g * amplitude[None, :]).astype(jnp.bfloat16)
    local_real = transposed_product(root_real, root_real) + transposed_product(root_imag, root_imag)
    skewed = transposed_product(root_imag, root_real)
    return (local_real, skewed - skewed.T)


def coupled_parts(real_g, imag_g, coupling):
    return (
        product(real_g, coupling).astype(jnp.bfloat16),
        product(imag_g, coupling).astype(jnp.bfloat16),
    )


def advance(local_pair, coupled_pair, carried_in):
    coupled_real, coupled_imag = coupled_pair
    prev_real = carried_in[0]
    prev_imag = carried_in[1]
    carried_real = (product(coupled_real, prev_real) - product(coupled_imag, prev_imag)).astype(
        jnp.bfloat16
    )
    carried_imag = (product(coupled_real, prev_imag) + product(coupled_imag, prev_real)).astype(
        jnp.bfloat16
    )
    new_real = (
        local_pair[0]
        + transposed_product(carried_real, coupled_real)
        + transposed_product(carried_imag, coupled_imag)
    )
    new_imag = (
        local_pair[1]
        + transposed_product(carried_imag, coupled_real)
        - transposed_product(carried_real, coupled_imag)
    )
    return jnp.stack([new_real.astype(jnp.bfloat16), new_imag.astype(jnp.bfloat16)])


def body(retarded, scatter_root, coupling, source_index, kernel_weight):
    points_dev = retarded.shape[1]
    states = retarded.shape[3]
    groups = lax.axis_size("ek")
    total_points = points_dev * groups
    row_count = states // groups
    kernel = build_kernel(source_index, kernel_weight, total_points)
    local_terms = []
    coupled_terms = []
    lesser = []
    for member in range(points_dev):
        real_g = retarded[0, member, 0]
        imag_g = retarded[0, member, 1]
        local_pair = local_parts(real_g, imag_g, scatter_root[0, member])
        local_terms.append(local_pair)
        coupled_terms.append(coupled_parts(real_g, imag_g, coupling))
        lesser.append(
            jnp.stack([local_pair[0].astype(jnp.bfloat16), local_pair[1].astype(jnp.bfloat16)])
        )
    carried = shifted(jnp.stack(lesser), "per", 1)
    lesser = [
        advance(local_terms[member], coupled_terms[member], carried[member])
        for member in range(points_dev)
    ]
    stacked = jnp.stack(lesser)[None]
    regrouped = lax.all_to_all(stacked, "ek", split_axis=3, concat_axis=1, tiled=True)
    summed = product(kernel, regrouped.reshape(total_points, -1))
    return summed.astype(jnp.bfloat16).reshape(1, total_points, 2, row_count, states)


SUB = 16
MESH = pl.DeviceIdType.MESH


def fused(
    groups,
    retarded,
    scatter,
    coupling,
    index_ref,
    weight_ref,
    out,
    green,
    stack,
    pair,
    moved,
    local,
    lesser,
    before,
    received,
    result,
    spread,
    load_sem,
    self_sem,
    send_sem,
    recv_sem,
    hand_sem,
    take_sem,
    out_sem,
):
    me = lax.axis_index("ek")
    period = lax.axis_index("per")
    points = green.shape[0]
    states = green.shape[2]
    rows = states // groups
    half = groups // 2
    total = points * groups
    tile = states // 2

    def load(member, part):
        return pltpu.make_async_copy(
            retarded.at[0, member, part], green.at[member, part], load_sem.at[member, part]
        )

    for member in range(points):
        for part in range(2):
            load(member, part).start()

    barrier = pltpu.get_barrier_semaphore()
    for step in range(1, groups):
        pl.semaphore_signal(
            barrier, inc=1, device_id={"ek": (me + step) % groups}, device_id_type=MESH
        )
    pl.semaphore_signal(barrier, inc=1, device_id={"per": 1 - period}, device_id_type=MESH)

    def targets():
        upper = me // half
        place = me % half
        found = [((upper + 1) % 2) * half + (place + step) % half for step in range(half)]
        return found + [upper * half + (place + step) % half for step in range(1, half)]

    def band(target):
        return pl.ds(pl.multiple_of(target * rows, SUB), rows)

    def send(member, part, slot, target):
        return pltpu.make_async_remote_copy(
            src_ref=lesser.at[member, part, band(target), :],
            dst_ref=received.at[me * points + member, part],
            send_sem=send_sem.at[member, part, slot],
            recv_sem=recv_sem.at[me * points + member, part],
            device_id={"ek": target},
            device_id_type=MESH,
        )

    def keep(member, part):
        return pltpu.make_async_copy(
            lesser.at[member, part, band(me), :],
            received.at[me * points + member, part],
            self_sem.at[member, part],
        )

    def hand(member):
        return pltpu.make_async_remote_copy(
            src_ref=lesser.at[member],
            dst_ref=before.at[member],
            send_sem=hand_sem.at[member],
            recv_sem=take_sem.at[member],
            device_id={"per": 1 - period},
            device_id_type=MESH,
        )

    def send_all(member):
        for part in range(2):
            for slot, target in enumerate(targets()):
                send(member, part, slot, target).start()
            keep(member, part).start()

    def tiles(body):
        for part in range(2):

            @pl.loop(0, 2)
            def _(at):
                body(part, pl.ds(pl.multiple_of(at * tile, SUB), tile), pl.ds(pl.multiple_of(part * states + at * tile, SUB), tile))

    def find_local(member):
        for part in range(2):
            load(member, part).wait()
        scale = scatter[0, pl.ds(member, 1), :]
        real = (green[member, 0].astype(jnp.float32) * scale).astype(jnp.bfloat16)
        imag = (green[member, 1].astype(jnp.float32) * scale).astype(jnp.bfloat16)
        stack[:states, :states] = real
        stack[states:, states:] = -real
        stack[:states, states:] = imag
        stack[states:, :states] = imag

        def one(part, rows_at, stacked_at):
            value = transposed_product(stack[stacked_at, :], stack[:states, :])
            local[member, part, rows_at, :] = value
            lesser[member, part, rows_at, :] = value.astype(jnp.bfloat16)

        tiles(one)

    def find_coupled(member):
        def one(part, rows_at, stacked_at):
            value = product(green[member, part, rows_at, :], coupling[...]).astype(jnp.bfloat16)
            if part == 0:
                pair[member, rows_at, :states] = value
                pair[member, pl.ds(stacked_at.start + states, tile), states:] = value
            else:
                pair[member, pl.ds(stacked_at.start - states, tile), states:] = -value
                pair[member, stacked_at, :states] = value

        tiles(one)

    def advance_point(member):
        def carry(part, rows_at, stacked_at):
            value = (
                product(pair[member, stacked_at, :states], before[member, 0])
                + product(pair[member, stacked_at, states:], before[member, 1])
            ).astype(jnp.bfloat16)
            if part == 0:
                moved[rows_at, states:] = value
                moved[pl.ds(stacked_at.start + states, tile), :states] = -value
            else:
                moved[rows_at, :states] = value
                moved[stacked_at, states:] = value

        tiles(carry)

        def close(part, rows_at, stacked_at):
            value = local[member, part, rows_at, :] + transposed_product(
                moved[stacked_at, :], pair[member, states:, :]
            )
            lesser[member, part, rows_at, :] = value.astype(jnp.bfloat16)

        tiles(close)

    find_local(0)
    pl.semaphore_wait(barrier, groups)

    @pl.when(period == 0)
    def _():
        hand(0).start()
        send_all(0)

    @pl.loop(1, points)
    def _(member):
        find_local(member)

        @pl.when(period == 0)
        def _():
            hand(member).start()
            send_all(member)

    @pl.when(period == 1)
    def _():
        @pl.loop(0, points)
        def _(member):
            find_coupled(member)
            hand(member).wait_recv()
            advance_point(member)
            send_all(member)

    source = index_ref[...]
    weight = weight_ref[...]
    column = lax.broadcasted_iota(jnp.int32, (total, total), 1)
    matrix = jnp.zeros((total, total), jnp.float32)
    for tap in range(source.shape[1]):
        matrix = matrix + jnp.where(
            source[:, tap : tap + 1] == column, weight[:, tap : tap + 1], 0.0
        )
    matrix = matrix.astype(jnp.bfloat16)
    long = total * SUB
    expand = jnp.where(
        lax.broadcasted_iota(jnp.int32, (long, total), 0) // SUB
        == lax.broadcasted_iota(jnp.int32, (long, total), 1),
        1.0,
        0.0,
    ).astype(jnp.bfloat16)
    wide = transposed_product(product(expand, matrix).astype(jnp.bfloat16), expand)
    same = (
        lax.broadcasted_iota(jnp.int32, (long, long), 0) % SUB
        == lax.broadcasted_iota(jnp.int32, (long, long), 1) % SUB
    )
    spread[...] = jnp.where(same, wide, 0.0).astype(jnp.bfloat16)

    def store(part):
        return pltpu.make_async_copy(result.at[part], out.at[0, :, part], out_sem.at[part])

    @pl.loop(0, points)
    def _(member):
        for part in range(2):
            keep(member, part).wait()

    for part in range(2):

        @pl.loop(1, groups)
        def _(step):
            other = (me + step) % groups

            @pl.loop(0, points)
            def _(member):
                pltpu.make_async_remote_copy(
                    src_ref=lesser.at[member, part, band(other), :],
                    dst_ref=received.at[other * points + member, part],
                    send_sem=send_sem.at[member, part, 0],
                    recv_sem=recv_sem.at[other * points + member, part],
                    device_id={"ek": other},
                    device_id_type=MESH,
                ).wait_recv()

        @pl.loop(0, rows // SUB)
        def _(at):
            span = pl.ds(pl.multiple_of(at * SUB, SUB), SUB)
            value = product(spread[...], received[:, part, span, :].reshape(long, states))
            result[part, :, span, :] = value.astype(jnp.bfloat16).reshape(total, SUB, states)

        store(part).start()

    @pl.loop(0, points)
    def _(member):
        for part in range(2):
            for slot, target in enumerate(targets()):
                send(member, part, slot, target).wait_send()

        @pl.when(period == 0)
        def _():
            hand(member).wait_send()

    for part in range(2):
        store(part).wait()


def fused_body(groups, retarded, scatter_root, coupling, source_index, kernel_weight):
    points = retarded.shape[1]
    states = retarded.shape[3]
    rows = states // groups
    total = points * groups
    dma = pltpu.SemaphoreType.DMA
    wide = jnp.bfloat16
    whole = pl.BlockSpec(memory_space=pltpu.VMEM)
    return pl.pallas_call(
        functools.partial(fused, groups),
        out_shape=jax.ShapeDtypeStruct((1, total, 2, rows, states), wide),
        in_specs=[pl.BlockSpec(memory_space=pl.ANY), whole, whole, whole, whole],
        out_specs=pl.BlockSpec(memory_space=pl.ANY),
        scratch_shapes=[
            pltpu.VMEM((points, 2, states, states), wide),
            pltpu.VMEM((2 * states, 2 * states), wide),
            pltpu.VMEM((points, 2 * states, 2 * states), wide),
            pltpu.VMEM((2 * states, 2 * states), wide),
            pltpu.VMEM((points, 2, states, states), jnp.float32),
            pltpu.VMEM((points, 2, states, states), wide),
            pltpu.VMEM((points, 2, states, states), wide),
            pltpu.VMEM((total, 2, rows, states), wide),
            pltpu.VMEM((2, total, rows, states), wide),
            pltpu.VMEM((total * SUB, total * SUB), wide),
            dma((points, 2)),
            dma((points, 2)),
            dma((points, 2, groups - 1)),
            dma((total, 2)),
            dma((points,)),
            dma((points,)),
            dma((2,)),
        ],
        compiler_params=pltpu.CompilerParams(
            collective_id=0, has_side_effects=True, vmem_limit_bytes=60 * 1024 * 1024
        ),
    )(retarded, scatter_root, coupling, source_index, kernel_weight)


def solution(mesh):
    groups = mesh.shape["ek"]

    def chosen(retarded, *others):
        states = retarded.shape[3]
        fits = states % (groups * SUB) == 0 and mesh.shape["per"] == 2 and groups % 2 == 0
        if fits:
            return fused_body(groups, retarded, *others)
        return body(retarded, *others)

    in_specs = (
        P("per", ("grp", "ek"), None, None, None),
        P("per", ("grp", "ek"), None),
        P(),
        P(),
        P(),
    )
    out_specs = P("per", "grp", None, "ek", None)
    return jax.shard_map(chosen, mesh=mesh, in_specs=in_specs, out_specs=out_specs, check_vma=False)
```

```python
import functools
import jax
import jax.numpy as jnp
from jax import lax
from jax.experimental import pallas as pl
from jax.experimental.pallas import tpu as pltpu
from jax.sharding import PartitionSpec as P


def shifted(array, axis, by):
    size = lax.axis_size(axis)
    pairs = [(i, i + by) for i in range(size) if 0 <= i + by < size]
    return lax.ppermute(array, axis, pairs)


def product(former, latter):
    return jnp.dot(former, latter, preferred_element_type=jnp.float32)


def transposed_product(former, latter):
    return lax.dot_general(
        former, latter, (((1,), (1,)), ((), ())), preferred_element_type=jnp.float32
    )


def build_kernel(source_index, kernel_weight, total_points):
    targets = jnp.arange(total_points, dtype=jnp.int32)
    matches = (source_index[:, :, None] == targets[None, None, :]).astype(jnp.float32)
    return jnp.sum(kernel_weight[:, :, None] * matches, axis=1).astype(jnp.bfloat16)


def local_parts(real_g, imag_g, amplitude):
    root_real = (real_g * amplitude[None, :]).astype(jnp.bfloat16)
    root_imag = (imag_g * amplitude[None, :]).astype(jnp.bfloat16)
    local_real = transposed_product(root_real, root_real) + transposed_product(root_imag, root_imag)
    skewed = transposed_product(root_imag, root_real)
    return (local_real, skewed - skewed.T)


def coupled_parts(real_g, imag_g, coupling):
    return (
        product(real_g, coupling).astype(jnp.bfloat16),
        product(imag_g, coupling).astype(jnp.bfloat16),
    )


def advance(local_pair, coupled_pair, carried_in):
    coupled_real, coupled_imag = coupled_pair
    prev_real = carried_in[0]
    prev_imag = carried_in[1]
    carried_real = (product(coupled_real, prev_real) - product(coupled_imag, prev_imag)).astype(
        jnp.bfloat16
    )
    carried_imag = (product(coupled_real, prev_imag) + product(coupled_imag, prev_real)).astype(
        jnp.bfloat16
    )
    new_real = (
        local_pair[0]
        + transposed_product(carried_real, coupled_real)
        + transposed_product(carried_imag, coupled_imag)
    )
    new_imag = (
        local_pair[1]
        + transposed_product(carried_imag, coupled_real)
        - transposed_product(carried_real, coupled_imag)
    )
    return jnp.stack([new_real.astype(jnp.bfloat16), new_imag.astype(jnp.bfloat16)])


def body(retarded, scatter_root, coupling, source_index, kernel_weight):
    points_dev = retarded.shape[1]
    states = retarded.shape[3]
    groups = lax.axis_size("ek")
    total_points = points_dev * groups
    row_count = states // groups
    kernel = build_kernel(source_index, kernel_weight, total_points)
    local_terms = []
    coupled_terms = []
    lesser = []
    for member in range(points_dev):
        real_g = retarded[0, member, 0]
        imag_g = retarded[0, member, 1]
        local_pair = local_parts(real_g, imag_g, scatter_root[0, member])
        local_terms.append(local_pair)
        coupled_terms.append(coupled_parts(real_g, imag_g, coupling))
        lesser.append(
            jnp.stack([local_pair[0].astype(jnp.bfloat16), local_pair[1].astype(jnp.bfloat16)])
        )
    carried = shifted(jnp.stack(lesser), "per", 1)
    lesser = [
        advance(local_terms[member], coupled_terms[member], carried[member])
        for member in range(points_dev)
    ]
    stacked = jnp.stack(lesser)[None]
    regrouped = lax.all_to_all(stacked, "ek", split_axis=3, concat_axis=1, tiled=True)
    summed = product(kernel, regrouped.reshape(total_points, -1))
    return summed.astype(jnp.bfloat16).reshape(1, total_points, 2, row_count, states)


SUB = 16
LIMIT = 48
MESH = pl.DeviceIdType.MESH


def fused(
    groups,
    retarded,
    scatter,
    coupling_ref,
    index_ref,
    weight_ref,
    out,
    green,
    coupling,
    stack,
    pair,
    moved,
    local,
    lesser,
    before,
    received,
    result,
    spread,
    load_sem,
    coupling_sem,
    self_sem,
    send_sem,
    recv_sem,
    hand_sem,
    take_sem,
    out_sem,
):
    me = lax.axis_index("ek")
    period = lax.axis_index("per")
    points = green.shape[0]
    states = green.shape[2]
    rows = states // groups
    half = groups // 2
    total = points * groups
    tile = states // 2

    def load(member, part):
        return pltpu.make_async_copy(
            retarded.at[0, member, part], green.at[member, part], load_sem.at[member, part]
        )

    for member in range(points):
        for part in range(2):
            load(member, part).start()
    fetch = pltpu.make_async_copy(coupling_ref, coupling, coupling_sem)
    fetch.start()

    barrier = pltpu.get_barrier_semaphore()
    for step in range(1, groups):
        pl.semaphore_signal(
            barrier, inc=1, device_id={"ek": (me + step) % groups}, device_id_type=MESH
        )
    pl.semaphore_signal(barrier, inc=1, device_id={"per": 1 - period}, device_id_type=MESH)

    upper = me // half
    place = me % half

    def band(target):
        return pl.ds(pl.multiple_of(target * rows, SUB), rows)

    def send(member, part, slot, target):
        return pltpu.make_async_remote_copy(
            src_ref=lesser.at[member, part, band(target), :],
            dst_ref=received.at[me * points + member, part],
            send_sem=send_sem.at[member, part, slot],
            recv_sem=recv_sem.at[me * points + member, part],
            device_id={"ek": target},
            device_id_type=MESH,
        )

    def keep(member, part):
        return pltpu.make_async_copy(
            lesser.at[member, part, band(me), :],
            received.at[me * points + member, part],
            self_sem.at[member, part],
        )

    def hand(member):
        return pltpu.make_async_remote_copy(
            src_ref=lesser.at[member],
            dst_ref=before.at[member],
            send_sem=hand_sem.at[member],
            recv_sem=take_sem.at[member],
            device_id={"per": 1 - period},
            device_id_type=MESH,
        )

    def send_tile(member, part, at):
        for step in range(half):
            target = at * half + (place + step) % half

            @pl.when(target != me)
            def _():
                send(member, part, target, target).start()

            @pl.when(target == me)
            def _():
                keep(member, part).start()

    def tiles(body, first, after=None):
        for part in range(2):

            @pl.loop(0, 2)
            def _(step):
                at = (first + step) % 2
                start = at * tile
                body(
                    part,
                    pl.ds(pl.multiple_of(start, SUB), tile),
                    pl.ds(pl.multiple_of(part * states + start, SUB), tile),
                )
                if after is not None:
                    after(part, at)

    def find_local(member, first):
        for part in range(2):
            load(member, part).wait()
        scale = scatter[0, pl.ds(member, 1), :]
        real = (green[member, 0].astype(jnp.float32) * scale).astype(jnp.bfloat16)
        imag = (green[member, 1].astype(jnp.float32) * scale).astype(jnp.bfloat16)
        stack[:states, :states] = real
        stack[states:, states:] = -real
        stack[:states, states:] = imag
        stack[states:, :states] = imag

        def one(part, rows_at, stacked_at):
            value = transposed_product(stack[stacked_at, :], stack[:states, :])
            local[member, part, rows_at, :] = value
            lesser[member, part, rows_at, :] = value.astype(jnp.bfloat16)

        def leave(part, at):
            @pl.when(period == 0)
            def _():
                send_tile(member, part, at)

        tiles(one, first, leave)

    def find_coupled(member):
        def one(part, rows_at, stacked_at):
            value = product(green[member, part, rows_at, :], coupling[...]).astype(jnp.bfloat16)
            if part == 0:
                pair[member, rows_at, :states] = value
                pair[member, pl.ds(stacked_at.start + states, tile), states:] = value
            else:
                pair[member, pl.ds(stacked_at.start - states, tile), states:] = -value
                pair[member, stacked_at, :states] = value

        tiles(one, 0)

    def advance_point(member):
        def carry(part, rows_at, stacked_at):
            value = (
                product(pair[member, stacked_at, :states], before[member, 0])
                + product(pair[member, stacked_at, states:], before[member, 1])
            ).astype(jnp.bfloat16)
            if part == 0:
                moved[rows_at, states:] = value
                moved[pl.ds(stacked_at.start + states, tile), :states] = -value
            else:
                moved[rows_at, :states] = value
                moved[stacked_at, states:] = value

        tiles(carry, 0)

        def close(part, rows_at, stacked_at):
            value = local[member, part, rows_at, :] + transposed_product(
                moved[stacked_at, :], pair[member, states:, :]
            )
            lesser[member, part, rows_at, :] = value.astype(jnp.bfloat16)

        tiles(close, upper, functools.partial(send_tile, member))

    fetch.wait()
    pl.semaphore_wait(barrier, groups)

    def give(member):
        @pl.when(period == 0)
        def _():
            hand(member).start()

    find_local(0, 1 - upper)
    give(0)

    @pl.loop(1, points)
    def _(member):
        find_local(member, upper)
        give(member)

    @pl.when(period == 1)
    def _():
        @pl.loop(0, points)
        def _(member):
            find_coupled(member)
            hand(member).wait_recv()
            advance_point(member)

    source = index_ref[...]
    weight = weight_ref[...]
    column = lax.broadcasted_iota(jnp.int32, (total, total), 1)
    matrix = jnp.zeros((total, total), jnp.float32)
    for tap in range(source.shape[1]):
        matrix = matrix + jnp.where(
            source[:, tap : tap + 1] == column, weight[:, tap : tap + 1], 0.0
        )
    matrix = matrix.astype(jnp.bfloat16)
    long = total * SUB
    expand = jnp.where(
        lax.broadcasted_iota(jnp.int32, (long, total), 0) // SUB
        == lax.broadcasted_iota(jnp.int32, (long, total), 1),
        1.0,
        0.0,
    ).astype(jnp.bfloat16)
    wide = transposed_product(product(expand, matrix).astype(jnp.bfloat16), expand)
    same = (
        lax.broadcasted_iota(jnp.int32, (long, long), 0) % SUB
        == lax.broadcasted_iota(jnp.int32, (long, long), 1) % SUB
    )
    spread[...] = jnp.where(same, wide, 0.0).astype(jnp.bfloat16)

    def store(part):
        return pltpu.make_async_copy(result.at[part], out.at[0, :, part], out_sem.at[part])

    @pl.loop(0, points)
    def _(member):
        for part in range(2):
            keep(member, part).wait()

    for part in range(2):

        @pl.loop(1, groups)
        def _(step):
            other = (me + step) % groups

            @pl.loop(0, points)
            def _(member):
                pltpu.make_async_remote_copy(
                    src_ref=lesser.at[member, part, band(other), :],
                    dst_ref=received.at[other * points + member, part],
                    send_sem=send_sem.at[member, part, 0],
                    recv_sem=recv_sem.at[other * points + member, part],
                    device_id={"ek": other},
                    device_id_type=MESH,
                ).wait_recv()

        @pl.loop(0, rows // SUB)
        def _(at):
            span = pl.ds(pl.multiple_of(at * SUB, SUB), SUB)
            value = product(spread[...], received[:, part, span, :].reshape(long, states))
            result[part, :, span, :] = value.astype(jnp.bfloat16).reshape(total, SUB, states)

        store(part).start()

    @pl.loop(0, points)
    def _(member):
        for part in range(2):
            for step in range(1, groups):
                target = (me + step) % groups
                send(member, part, target, target).wait_send()

        @pl.when(period == 0)
        def _():
            hand(member).wait_send()

    for part in range(2):
        store(part).wait()


def fused_body(groups, retarded, scatter_root, coupling, source_index, kernel_weight):
    points = retarded.shape[1]
    states = retarded.shape[3]
    rows = states // groups
    total = points * groups
    dma = pltpu.SemaphoreType.DMA
    wide = jnp.bfloat16
    whole = pl.BlockSpec(memory_space=pltpu.VMEM)
    return pl.pallas_call(
        functools.partial(fused, groups),
        out_shape=jax.ShapeDtypeStruct((1, total, 2, rows, states), wide),
        in_specs=[
            pl.BlockSpec(memory_space=pl.ANY),
            whole,
            pl.BlockSpec(memory_space=pl.ANY),
            whole,
            whole,
        ],
        out_specs=pl.BlockSpec(memory_space=pl.ANY),
        scratch_shapes=[
            pltpu.VMEM((points, 2, states, states), wide),
            pltpu.VMEM((states, states), wide),
            pltpu.VMEM((2 * states, 2 * states), wide),
            pltpu.VMEM((points, 2 * states, 2 * states), wide),
            pltpu.VMEM((2 * states, 2 * states), wide),
            pltpu.VMEM((points, 2, states, states), jnp.float32),
            pltpu.VMEM((points, 2, states, states), wide),
            pltpu.VMEM((points, 2, states, states), wide),
            pltpu.VMEM((total, 2, rows, states), wide),
            pltpu.VMEM((2, total, rows, states), wide),
            pltpu.VMEM((total * SUB, total * SUB), wide),
            dma((points, 2)),
            dma,
            dma((points, 2)),
            dma((points, 2, groups)),
            dma((total, 2)),
            dma((points,)),
            dma((points,)),
            dma((2,)),
        ],
        compiler_params=pltpu.CompilerParams(
            collective_id=0, has_side_effects=True, vmem_limit_bytes=LIMIT * 1024 * 1024
        ),
    )(retarded, scatter_root, coupling, source_index, kernel_weight)


def solution(mesh):
    groups = mesh.shape["ek"]

    def chosen(retarded, *others):
        states = retarded.shape[3]
        fits = states % (groups * SUB) == 0 and mesh.shape["per"] == 2 and groups % 2 == 0
        if fits:
            return fused_body(groups, retarded, *others)
        return body(retarded, *others)

    in_specs = (
        P("per", ("grp", "ek"), None, None, None),
        P("per", ("grp", "ek"), None),
        P(),
        P(),
        P(),
    )
    out_specs = P("per", "grp", None, "ek", None)
    return jax.shard_map(chosen, mesh=mesh, in_specs=in_specs, out_specs=out_specs, check_vma=False)
```

```python
import functools
import jax
import jax.numpy as jnp
from jax import lax
from jax.experimental import pallas as pl
from jax.experimental.pallas import tpu as pltpu
from jax.sharding import PartitionSpec as P


def shifted(array, axis, by):
    size = lax.axis_size(axis)
    pairs = [(i, i + by) for i in range(size) if 0 <= i + by < size]
    return lax.ppermute(array, axis, pairs)


def product(former, latter):
    return jnp.dot(former, latter, preferred_element_type=jnp.float32)


def transposed_product(former, latter):
    return lax.dot_general(
        former, latter, (((1,), (1,)), ((), ())), preferred_element_type=jnp.float32
    )


def build_kernel(source_index, kernel_weight, total_points):
    targets = jnp.arange(total_points, dtype=jnp.int32)
    matches = (source_index[:, :, None] == targets[None, None, :]).astype(jnp.float32)
    return jnp.sum(kernel_weight[:, :, None] * matches, axis=1).astype(jnp.bfloat16)


def local_parts(real_g, imag_g, amplitude):
    root_real = (real_g * amplitude[None, :]).astype(jnp.bfloat16)
    root_imag = (imag_g * amplitude[None, :]).astype(jnp.bfloat16)
    local_real = transposed_product(root_real, root_real) + transposed_product(root_imag, root_imag)
    skewed = transposed_product(root_imag, root_real)
    return (local_real, skewed - skewed.T)


def coupled_parts(real_g, imag_g, coupling):
    return (
        product(real_g, coupling).astype(jnp.bfloat16),
        product(imag_g, coupling).astype(jnp.bfloat16),
    )


def advance(local_pair, coupled_pair, carried_in):
    coupled_real, coupled_imag = coupled_pair
    prev_real = carried_in[0]
    prev_imag = carried_in[1]
    carried_real = (product(coupled_real, prev_real) - product(coupled_imag, prev_imag)).astype(
        jnp.bfloat16
    )
    carried_imag = (product(coupled_real, prev_imag) + product(coupled_imag, prev_real)).astype(
        jnp.bfloat16
    )
    new_real = (
        local_pair[0]
        + transposed_product(carried_real, coupled_real)
        + transposed_product(carried_imag, coupled_imag)
    )
    new_imag = (
        local_pair[1]
        + transposed_product(carried_imag, coupled_real)
        - transposed_product(carried_real, coupled_imag)
    )
    return jnp.stack([new_real.astype(jnp.bfloat16), new_imag.astype(jnp.bfloat16)])


def body(retarded, scatter_root, coupling, source_index, kernel_weight):
    points_dev = retarded.shape[1]
    states = retarded.shape[3]
    groups = lax.axis_size("ek")
    total_points = points_dev * groups
    row_count = states // groups
    kernel = build_kernel(source_index, kernel_weight, total_points)
    local_terms = []
    coupled_terms = []
    lesser = []
    for member in range(points_dev):
        real_g = retarded[0, member, 0]
        imag_g = retarded[0, member, 1]
        local_pair = local_parts(real_g, imag_g, scatter_root[0, member])
        local_terms.append(local_pair)
        coupled_terms.append(coupled_parts(real_g, imag_g, coupling))
        lesser.append(
            jnp.stack([local_pair[0].astype(jnp.bfloat16), local_pair[1].astype(jnp.bfloat16)])
        )
    carried = shifted(jnp.stack(lesser), "per", 1)
    lesser = [
        advance(local_terms[member], coupled_terms[member], carried[member])
        for member in range(points_dev)
    ]
    stacked = jnp.stack(lesser)[None]
    regrouped = lax.all_to_all(stacked, "ek", split_axis=3, concat_axis=1, tiled=True)
    summed = product(kernel, regrouped.reshape(total_points, -1))
    return summed.astype(jnp.bfloat16).reshape(1, total_points, 2, row_count, states)


SUB = 16
LIMIT = 58
MESH = pl.DeviceIdType.MESH


def fused(
    groups,
    retarded,
    scatter_ref,
    coupling_ref,
    index_ref,
    weight_ref,
    received,
    spread,
    green,
    coupling,
    scatter,
    index,
    weight,
    stack,
    pair,
    moved,
    local,
    lesser,
    before,
    load_sem,
    small_sem,
    self_sem,
    send_sem,
    recv_sem,
    hand_sem,
    take_sem,
):
    me = lax.axis_index("ek")
    period = lax.axis_index("per")
    points = green.shape[0]
    states = green.shape[2]
    rows = states // groups
    half = groups // 2
    total = points * groups
    tile = states // 2

    def load(member, part):
        return pltpu.make_async_copy(
            retarded.at[0, member, part], green.at[member, part], load_sem.at[member, part]
        )

    def fetch(at):
        origin, held = (
            (scatter_ref, scatter),
            (coupling_ref, coupling),
            (index_ref, index),
            (weight_ref, weight),
        )[at]
        return pltpu.make_async_copy(origin, held, small_sem.at[at])

    fetch(0).start()
    for member in range(points):
        for part in range(2):
            load(member, part).start()
    for at in range(1, 4):
        fetch(at).start()

    barrier = pltpu.get_barrier_semaphore()
    for step in range(1, groups):
        pl.semaphore_signal(
            barrier, inc=1, device_id={"ek": (me + step) % groups}, device_id_type=MESH
        )
    pl.semaphore_signal(barrier, inc=1, device_id={"per": 1 - period}, device_id_type=MESH)

    upper = me // half
    place = me % half

    def band(target):
        return pl.ds(pl.multiple_of(target * rows, SUB), rows)

    def send(member, part, slot, target):
        return pltpu.make_async_remote_copy(
            src_ref=lesser.at[member, part, band(target), :],
            dst_ref=received.at[me * points + member, part],
            send_sem=send_sem.at[member, part, slot],
            recv_sem=recv_sem.at[me * points + member, part],
            device_id={"ek": target},
            device_id_type=MESH,
        )

    def keep(member, part):
        return pltpu.make_async_copy(
            lesser.at[member, part, band(me), :],
            received.at[me * points + member, part],
            self_sem.at[member, part],
        )

    def hand(member):
        return pltpu.make_async_remote_copy(
            src_ref=lesser.at[member],
            dst_ref=before.at[member],
            send_sem=hand_sem.at[member],
            recv_sem=take_sem.at[member],
            device_id={"per": 1 - period},
            device_id_type=MESH,
        )

    def send_tile(member, part, at):
        for step in range(half):
            target = at * half + (place + step) % half

            @pl.when(target != me)
            def _():
                send(member, part, target, target).start()

            @pl.when(target == me)
            def _():
                keep(member, part).start()

    def tiles(body, first, after=None):
        for part in range(2):

            @pl.loop(0, 2)
            def _(step):
                at = (first + step) % 2
                start = at * tile
                body(
                    part,
                    pl.ds(pl.multiple_of(start, SUB), tile),
                    pl.ds(pl.multiple_of(part * states + start, SUB), tile),
                )
                if after is not None:
                    after(part, at)

    def find_local(member, first):
        for part in range(2):
            load(member, part).wait()
        scale = scatter[0, pl.ds(member, 1), :]
        real = (green[member, 0].astype(jnp.float32) * scale).astype(jnp.bfloat16)
        imag = (green[member, 1].astype(jnp.float32) * scale).astype(jnp.bfloat16)
        stack[:states, :states] = real
        stack[states:, states:] = -real
        stack[:states, states:] = imag
        stack[states:, :states] = imag

        def one(part, rows_at, stacked_at):
            value = transposed_product(stack[stacked_at, :], stack[:states, :])
            local[member, part, rows_at, :] = value
            lesser[member, part, rows_at, :] = value.astype(jnp.bfloat16)

        def leave(part, at):
            @pl.when(period == 0)
            def _():
                send_tile(member, part, at)

        tiles(one, first, leave)

    def find_coupled(member):
        def one(part, rows_at, stacked_at):
            value = product(green[member, part, rows_at, :], coupling[...]).astype(jnp.bfloat16)
            if part == 0:
                pair[member, rows_at, :states] = value
                pair[member, pl.ds(stacked_at.start + states, tile), states:] = value
            else:
                pair[member, pl.ds(stacked_at.start - states, tile), states:] = -value
                pair[member, stacked_at, :states] = value

        tiles(one, 0)

    def advance_point(member):
        def carry(part, rows_at, stacked_at):
            value = (
                product(pair[member, stacked_at, :states], before[member, 0])
                + product(pair[member, stacked_at, states:], before[member, 1])
            ).astype(jnp.bfloat16)
            if part == 0:
                moved[rows_at, states:] = value
                moved[pl.ds(stacked_at.start + states, tile), :states] = -value
            else:
                moved[rows_at, :states] = value
                moved[stacked_at, states:] = value

        tiles(carry, 0)

        def close(part, rows_at, stacked_at):
            value = local[member, part, rows_at, :] + transposed_product(
                moved[stacked_at, :], pair[member, states:, :]
            )
            lesser[member, part, rows_at, :] = value.astype(jnp.bfloat16)

        tiles(close, 1 - upper, functools.partial(send_tile, member))

    pl.semaphore_wait(barrier, groups)
    fetch(0).wait()
    fetch(1).wait()

    def give(member):
        @pl.when(period == 0)
        def _():
            hand(member).start()

    find_local(0, 1 - upper)
    give(0)

    @pl.loop(1, points)
    def _(member):
        find_local(member, 1 - upper)
        give(member)

    @pl.when(period == 1)
    def _():
        @pl.loop(0, points)
        def _(member):
            find_coupled(member)
            hand(member).wait_recv()
            advance_point(member)

    fetch(2).wait()
    fetch(3).wait()
    source = index[...]
    taps = weight[...]
    column = lax.broadcasted_iota(jnp.int32, (total, total), 1)
    matrix = jnp.zeros((total, total), jnp.float32)
    for tap in range(source.shape[1]):
        matrix = matrix + jnp.where(
            source[:, tap : tap + 1] == column, taps[:, tap : tap + 1], 0.0
        )
    matrix = matrix.astype(jnp.bfloat16)
    long = total * SUB
    expand = jnp.where(
        lax.broadcasted_iota(jnp.int32, (long, total), 0) // SUB
        == lax.broadcasted_iota(jnp.int32, (long, total), 1),
        1.0,
        0.0,
    ).astype(jnp.bfloat16)
    wide = transposed_product(product(expand, matrix).astype(jnp.bfloat16), expand)
    same = (
        lax.broadcasted_iota(jnp.int32, (long, long), 0) % SUB
        == lax.broadcasted_iota(jnp.int32, (long, long), 1) % SUB
    )
    spread[...] = jnp.where(same, wide, 0.0).astype(jnp.bfloat16)

    @pl.loop(0, points)
    def _(member):
        for part in range(2):
            keep(member, part).wait()

    for part in range(2):

        @pl.loop(1, groups)
        def _(step):
            other = (me + step) % groups

            @pl.loop(0, points)
            def _(member):
                pltpu.make_async_remote_copy(
                    src_ref=lesser.at[member, part, band(other), :],
                    dst_ref=received.at[other * points + member, part],
                    send_sem=send_sem.at[member, part, 0],
                    recv_sem=recv_sem.at[other * points + member, part],
                    device_id={"ek": other},
                    device_id_type=MESH,
                ).wait_recv()

    @pl.loop(0, points)
    def _(member):
        for part in range(2):
            for step in range(1, groups):
                target = (me + step) % groups
                send(member, part, target, target).wait_send()

        @pl.when(period == 0)
        def _():
            hand(member).wait_send()

def convolve(spread, received, out):
    total, _, sub, states = received.shape
    value = product(spread[...], received[:, 0].reshape(total * sub, states))
    out[0, :, 0] = value.astype(out.dtype).reshape(total, sub, states)


def fused_body(groups, retarded, scatter_root, coupling, source_index, kernel_weight):
    points = retarded.shape[1]
    states = retarded.shape[3]
    rows = states // groups
    total = points * groups
    dma = pltpu.SemaphoreType.DMA
    wide = jnp.bfloat16
    received, spread = pl.pallas_call(
        functools.partial(fused, groups),
        out_shape=[
            jax.ShapeDtypeStruct((total, 2, rows, states), wide),
            jax.ShapeDtypeStruct((total * SUB, total * SUB), wide),
        ],
        in_specs=[pl.BlockSpec(memory_space=pltpu.HBM)] * 5,
        out_specs=[
            pl.BlockSpec(memory_space=pl.ANY),
            pl.BlockSpec(memory_space=pltpu.VMEM),
        ],
        scratch_shapes=[
            pltpu.VMEM((points, 2, states, states), wide),
            pltpu.VMEM((states, states), wide),
            pltpu.VMEM(scatter_root.shape, jnp.float32),
            pltpu.VMEM(source_index.shape, jnp.int32),
            pltpu.VMEM(kernel_weight.shape, jnp.float32),
            pltpu.VMEM((2 * states, 2 * states), wide),
            pltpu.VMEM((points, 2 * states, 2 * states), wide),
            pltpu.VMEM((2 * states, 2 * states), wide),
            pltpu.VMEM((points, 2, states, states), jnp.float32),
            pltpu.VMEM((points, 2, states, states), wide),
            pltpu.VMEM((points, 2, states, states), wide),
            dma((points, 2)),
            dma((4,)),
            dma((points, 2)),
            dma((points, 2, groups)),
            dma((total, 2)),
            dma((points,)),
            dma((points,)),
        ],
        compiler_params=pltpu.CompilerParams(
            collective_id=0, has_side_effects=True, vmem_limit_bytes=LIMIT * 1024 * 1024
        ),
    )(retarded, scatter_root, coupling, source_index, kernel_weight)
    return pl.pallas_call(
        convolve,
        grid=(2, rows // SUB),
        out_shape=jax.ShapeDtypeStruct((1, total, 2, rows, states), wide),
        in_specs=[
            pl.BlockSpec((total * SUB, total * SUB), lambda part, at: (0, 0)),
            pl.BlockSpec((total, 1, SUB, states), lambda part, at: (0, part, at, 0)),
        ],
        out_specs=pl.BlockSpec((1, total, 1, SUB, states), lambda part, at: (0, 0, part, at, 0)),
    )(spread, received)


def solution(mesh):
    groups = mesh.shape["ek"]

    def chosen(retarded, *others):
        states = retarded.shape[3]
        fits = states % (groups * SUB) == 0 and mesh.shape["per"] == 2 and groups % 2 == 0
        if fits:
            return fused_body(groups, retarded, *others)
        return body(retarded, *others)

    in_specs = (
        P("per", ("grp", "ek"), None, None, None),
        P("per", ("grp", "ek"), None),
        P(),
        P(),
        P(),
    )
    out_specs = P("per", "grp", None, "ek", None)
    return jax.shard_map(chosen, mesh=mesh, in_specs=in_specs, out_specs=out_specs, check_vma=False)
```
